32 devices in a mesh: outer: 4 (over y, x), inner: 2 (over core), col: 4 (over z).
Axes of the slice: x: 2, y: 2, z: 4, core: 2. Of those that a mesh axis runs over, the one named last changes fastest.
Arguments:
- operator: bfloat16 [4096, 8192], P(('outer', 'inner'), 'col'), as said below
- test_matrix: bfloat16 [8192, 256], P('col'), may hold values from -6 to 6
Outputs:
- basis: float32 [4096, 256], P(('outer', 'inner'), 'col')
- factor: float32 [256, 256], replicated
The draws below stay inside these ranges and needn't reach their ends.
Inputs may be any that keep to these rules, and one draw needn't show every extreme that they name: Entries of the operator are of order 1 / sqrt(8192) times row and column scales between 0.5 and 4.
All inputs are finite; a program needn't handle non-finite values.
Results may differ from the reference program's by a relative error of at most 0.003.
Values may be sent and summed in bfloat16 or wider, within the bound.
A program may use at most 64 MiB of HBM per device.

```python
import jax
import jax.numpy as jnp
from jax import lax

N = 8192
K = 256
ROWS = 4096


def draw_operator(key, part):
    key_base = jax.random.fold_in(key, 11)
    key_rows = jax.random.fold_in(key, 12)
    key_cols = jax.random.fold_in(key, 13)
    position = jnp.arange(ROWS, dtype=jnp.float32).reshape(ROWS, 1) / ROWS
    row_scale = jnp.exp(position * jnp.log(3.0) + jax.random.uniform(key_rows, (ROWS, 1), jnp.float32, -0.25, 0.25))
    col_scale = jnp.exp(jax.random.uniform(key_cols, (1, N), jnp.float32, -0.35, 0.35))
    base = jax.random.normal(key_base, (ROWS, N), jnp.float32)
    return (base * row_scale * col_scale / jnp.sqrt(jnp.float32(N))).astype(jnp.bfloat16)


def block_scale(key, extent, shards, least, largest):
    loudness, own = 1.0, jax.random.fold_in(key, 6)
    for axis_at, parts in shards:
        draws = jnp.exp(jax.random.uniform(jax.random.fold_in(own, axis_at), (parts,), jnp.float32, least / len(shards), largest / len(shards)))
        loudness = loudness * jnp.repeat(draws, extent[axis_at] // parts).reshape([-1 if axis == axis_at else 1 for axis in range(len(extent))])
    return loudness


def scatter_about(stream_key, shape, deviation, most, shards=(), kind=jnp.bfloat16):
    factor_of = block_scale(stream_key, shape, shards, -0.22, 0.18) if shards else 1.0
    entries = jax.random.normal(stream_key, shape, jnp.float32) * deviation * factor_of
    return jnp.minimum(jnp.maximum(entries, -most), most).astype(kind)


def setup_inputs(seed: int = 0) -> dict:
    seeds = jax.random.split(jax.random.key(seed), 3)
    operator = draw_operator(jax.random.fold_in(seeds[2], 71), 0)
    test_matrix = scatter_about(seeds[1], (N, K), 1.0, 6.0, ((0, 4),))
    return dict(operator=operator, test_matrix=test_matrix)


def gram_of(matrix):
    return jnp.dot(matrix.T.astype(jnp.float32), matrix.astype(jnp.float32), precision=lax.Precision.HIGHEST, preferred_element_type=jnp.float32)

def right_solve(lower, matrix):
    return jax.scipy.linalg.solve_triangular(lower, matrix.T, lower=True).T

def reference(operator, test_matrix):
    sketch = jnp.dot(operator.astype(jnp.float32), test_matrix.astype(jnp.float32), preferred_element_type=jnp.float32).astype(jnp.bfloat16)
    total = jnp.dot(operator.T.astype(jnp.float32), sketch.astype(jnp.float32), preferred_element_type=jnp.float32)
    normal = (total * (N / ROWS)).astype(jnp.bfloat16)
    image = jnp.dot(operator.astype(jnp.float32), normal.astype(jnp.float32), preferred_element_type=jnp.float32)
    lower = jnp.linalg.cholesky(gram_of(image))
    orthonormal = right_solve(lower, image)
    root = jnp.sqrt(jnp.float32(ROWS))
    basis = orthonormal * root
    factor = lower.T / root
    return (basis, factor)
```

```python
import functools

import jax
import jax.numpy as jnp
from jax import lax
from jax.experimental import pallas as pl
from jax.experimental.pallas import tpu as pltpu
from jax.sharding import PartitionSpec as P

F32 = jnp.float32
BF16 = jnp.bfloat16
MESH = pl.DeviceIdType.MESH
HIGHEST = lax.Precision.HIGHEST
SPANS = 4
BLOCK = 32


def wide_sketch(half, flip):
    return flip == 1


def wide_image(flip):
    return False


def split(value):
    high = value.astype(BF16)
    rest = value - high.astype(F32)
    middle = rest.astype(BF16)
    low = (rest - middle.astype(F32)).astype(BF16)
    return high, middle, low


def eliminate(s_ref, w_ref):
    size = s_ref.shape[0]
    row = lax.broadcasted_iota(jnp.int32, (size, size), 0)
    col = lax.broadcasted_iota(jnp.int32, (size, size), 1)
    w_ref[...] = jnp.where(row == col, jnp.float32(1), jnp.float32(0))
    sub = lax.broadcasted_iota(jnp.int32, (8, 128), 0)
    wide = 128
    for start in range(0, size, BLOCK):
        rows = BLOCK // 8
        tiles = [(s_ref, t) for t in range(start // wide, size // wide)]
        tiles += [(w_ref, t) for t in range(0, start // wide + 1)]
        q = [[ref[start + 8 * g:start + 8 * g + 8, t * wide:(t + 1) * wide] for ref, t in tiles]
             for g in range(rows)]
        for p in range(rows):
            first = (start + 8 * p) % wide
            cs = [[jnp.broadcast_to(q[g][0][:, first + n:first + n + 1], (8, wide)) for n in range(8)]
                  for g in range(p, rows)]
            pivots = jnp.zeros((8, wide), F32)
            for n in range(8):
                pivot = jnp.broadcast_to(cs[0][n][n:n + 1], (8, wide))
                pivots = jnp.where(sub == n, pivot, pivots)
                inverse = 1.0 / pivot
                heads = {m: jnp.broadcast_to(cs[0][m][n:n + 1], (8, wide)) * inverse for m in range(n + 1, 8)}
                bodies = [jnp.broadcast_to(tile[n:n + 1], (8, wide)) * inverse for tile in q[p]]
                for g in range(p, rows):
                    weight = cs[g - p][n]
                    if g == p:
                        weight = jnp.where(sub > n, weight, 0.0)
                    for m in range(n + 1, 8):
                        cs[g - p][m] = cs[g - p][m] - weight * heads[m]
                    q[g] = [tile - weight * body for tile, body in zip(q[g], bodies)]
            scale = lax.rsqrt(pivots)
            q[p] = [tile * scale for tile in q[p]]
        for g in range(rows):
            for (ref, t), tile in zip(tiles, q[g]):
                ref[start + 8 * g:start + 8 * g + 8, t * wide:(t + 1) * wide] = tile
        done = start + BLOCK
        if done < size:
            block = jnp.concatenate([jnp.concatenate(q[g], axis=1) for g in range(rows)], axis=0)
            h, m, l = split(block)
            count = size // wide - start // wide
            base = (start // wide) * wide
            take = slice(done - base, count * wide) if (done - base) % wide == 0 else slice(0, count * wide)
            skip = done - base - (take.start or 0)
            left = jnp.concatenate([h, h, m, m, h, l], axis=0)[:, take]
            right = jnp.concatenate([h, m, h, m, l, h], axis=0)
            update = lax.dot_general(left, right, (((0,), (0,)), ((), ())), preferred_element_type=F32)[skip:]
            for at, (ref, t) in enumerate(tiles):
                lanes = slice(t * wide, (t + 1) * wide)
                ref[done:, lanes] = ref[done:, lanes] - update[:, at * wide:(at + 1) * wide]


def exact(left, right, left_dim, right_dim):
    return lax.dot_general(left, right, (((left_dim,), (right_dim,)), ((), ())),
                           precision=HIGHEST, preferred_element_type=F32)


def power_kernel(
    sizes, ratio, root, a_hbm, om_hbm, inverse_ref, im, factor_ref,
    a, om, p1, w1, r1, n1, sg, sk, p2, w2, r2, nt, p3, w3, r3, n3, x, gp, ra, gb, gf, s0_ref, s1_ref, w0_ref, w1_ref, w_ref,
    load_sem, pair_s, pair_v, s1, v1, s2, v2, s3, v3, s4, v4, s5, v5, s7, v7, s8, v8, s9, v9, sf, vf,
):
    outer, inner, cols = sizes
    chips = inner // 2
    groups = outer * chips
    o, i, c = lax.axis_index("outer"), lax.axis_index("inner"), lax.axis_index("col")
    k = lax.rem(i, 2)
    other = 1 - k
    chip = lax.div(i, 2)
    r = o * chips + chip
    partner = (o, chip * 2 + other, c)
    flips = range(1, cols)

    def col_peer(m):
        return jnp.bitwise_xor(c, m)

    def row_peer(s):
        return lax.rem(r + s, groups)

    def at_col(to, core):
        return (o, chip * 2 + core, to)

    def at_row(to, core):
        return (lax.div(to, chips), lax.rem(to, chips) * 2 + core, c)

    def copy_of(src, dst, ss, rs, to):
        return pltpu.make_async_remote_copy(
            src_ref=src, dst_ref=dst, send_sem=ss, recv_sem=rs, device_id=to, device_id_type=MESH
        )

    def send(src, dst, ss, rs, to):
        copy = copy_of(src, dst, ss, rs, to)
        copy.start()
        return copy

    def arrive(dst, rs):
        copy_of(dst, dst, rs, rs, partner).wait_recv()

    width = om.shape[1] // 2

    def lanes_of(h):
        return slice(h * width, (h + 1) * width)

    load_a = pltpu.make_async_copy(a_hbm, a.at[k], load_sem.at[0])
    load_a.start()
    load_om = [pltpu.make_async_copy(om_hbm.at[:, lanes_of(h)], om.at[:, lanes_of(h)], load_sem.at[1 + h]) for h in range(2)]
    for load in load_om:
        load.start()

    barrier = pltpu.get_barrier_semaphore()
    peers = [partner]
    for m in flips:
        peers += [at_col(col_peer(m), k), at_col(col_peer(m), other)]
    for s in range(1, groups):
        peers += [at_row(row_peer(s), k), at_row(row_peer(s), other)]
    for to in peers:
        pl.semaphore_signal(barrier, inc=1, device_id=to, device_id_type=MESH)
    load_a.wait()

    part = p1.shape[1] // cols
    own = pl.ds(pl.multiple_of(c * part, part), part)

    def rows_of(to):
        return pl.ds(pl.multiple_of(to * part, part), part)

    sends = []
    sums = []
    for h in range(2):
        load_om[h].wait()
        p1[h] = jnp.dot(a[k], om[:, lanes_of(h)], preferred_element_type=F32)
        if not all(wide_sketch(h, m) for m in flips):
            w1[h] = p1[h].astype(BF16)
        if h == 0:
            pl.semaphore_wait(barrier, len(peers))
        copies = []
        for n, m in enumerate(flips):
            if h == 1:
                sums[0][n].wait_send()
            to = col_peer(m)
            src, dst = (p1, r1) if wide_sketch(h, m) else (w1, n1)
            copies.append(send(src.at[h, rows_of(to)], dst.at[h, m - 1], s1.at[h, m - 1], v1.at[h, m - 1], at_col(to, k)))
        sums.append(copies)
        if h == 0:
            swap = send(a_hbm, a.at[k], pair_s.at[0], pair_v.at[0], partner)
    first_sums = sums
    for h in range(2):
        for copy in sums[h]:
            copy.wait_recv()
        total = p1[h, own]
        for m in flips:
            total = total + (r1[h, m - 1] if wide_sketch(h, m) else n1[h, m - 1].astype(F32))
        sg[h] = total.astype(BF16)
        for m in flips:
            sends.append(send(sg.at[h], sk.at[k, c], s2.at[h, m - 1], v2.at[k, m - 1], at_col(col_peer(m), h)))

        @pl.when(k == h)
        def _():
            sk[k, c] = sg[h]

        @pl.when(k != h)
        def _():
            send(sg.at[h], sk.at[k, c], pair_s.at[1], pair_v.at[1], partner)

    swap.wait()
    arrive(sk.at[other, c], pair_v.at[1])
    turned = []
    for j in range(2):
        for m in flips:
            arrive(sk.at[j, col_peer(m)], v2.at[j, m - 1])
        turned.append(jnp.concatenate([sk[j, to] for to in range(cols)], axis=0).astype(F32).T.astype(BF16))
    lanes = p2.shape[2]
    depth = p2.shape[3]
    sums = []
    for span in range(SPANS):
        at = slice(span * depth, (span + 1) * depth)
        normal = None
        for j in range(2):
            term = jnp.dot(turned[j], a[j, :, at], preferred_element_type=F32)
            normal = term if normal is None else normal + term
        for g in range(groups):
            p2[span, g] = normal[g * lanes:(g + 1) * lanes]
            w2[span, g] = normal[g * lanes:(g + 1) * lanes].astype(BF16)
        copies = []
        for s in range(1, groups):
            to = row_peer(s)
            copies.append(send(w2.at[span, to], r2.at[span, s - 1], s3.at[span, s - 1], v3.at[span, s - 1], at_row(to, k)))
        sums.append(copies)
    wholes = []
    for span in range(SPANS):
        for copy in sums[span]:
            copy.wait()
        total = p2[span, r]
        for s in range(1, groups):
            total = total + r2[span, s - 1].astype(F32)
        nt[span, r] = (total * ratio).astype(BF16)
        copies = []
        for s in range(1, groups):
            copies.append(send(nt.at[span, r], nt.at[span, r], s4.at[span, s - 1], v4.at[span, s - 1], at_row(row_peer(s), k)))
        wholes.append(copies)

    spans = []
    sums = []
    for span in range(SPANS):
        for copy in wholes[span]:
            copy.wait()
        if lanes % 16 == 0:
            spans.append(nt[span].reshape(groups * lanes, depth))
        else:
            spans.append(jnp.concatenate([nt[span, g].astype(F32) for g in range(groups)], axis=0).astype(BF16))
        for block in range(2):
            term = lax.dot_general(a[block, :, span * depth:(span + 1) * depth], spans[span],
                                   (((1,), (1,)), ((), ())), preferred_element_type=F32)
            if span > 0:
                term = p3[block] + term
            p3[block] = term
            if span < SPANS - 1:
                continue
            w3[block] = term.astype(BF16)
            copies = []
            for m in flips:
                to = col_peer(m)
                src, dst = (p3, r3) if wide_image(m) else (w3, n3)
                copies.append(send(src.at[block, rows_of(to)], dst.at[block, m - 1],
                                   s5.at[block, m - 1], v5.at[block, m - 1], at_col(to, k)))
            sums.append(copies)
    for block in range(2):
        for copy in sums[block]:
            copy.wait()
        total = p3[block, own]
        for m in flips:
            total = total + (r3[block, m - 1] if wide_image(m) else n3[block, m - 1].astype(F32))
        x[k, block] = total
    pair = send(x.at[k], x.at[k], pair_s.at[2], pair_v.at[2], partner)

    def image_copies(turns=(0, 1)):
        return [
            copy_of(x.at[k, core], im.at[c, k], s8.at[m - 1, n], v8.at[k, m - 1], at_col(col_peer(m), core))
            for m in flips for n, core in enumerate((k, other)) if n in turns
        ]

    piece = gp.shape[2]

    def gram(first, count):
        mine = x[k].reshape(2 * part, width)
        for n in range(count):
            full = exact(x[n].reshape(2 * part, width), mine, 0, 0)
            for to in range(groups):
                gp[to, n] = full[to * piece:(to + 1) * piece]
        some = slice(0, count)
        copies = []
        for s in range(1, groups):
            to = row_peer(s)
            copies.append(send(gp.at[to, some], ra.at[s - 1, some], s7.at[s - 1], v7.at[s - 1], at_row(to, k)))
        if first == 0:
            for copy in image_copies((0,)):
                copy.start()
        for copy in copies:
            copy.wait()
        total = gp[r, some]
        for s in range(1, groups):
            total = total + ra[s - 1, some]
        gb[c, some] = total
        copies = [send(gb.at[c, some], gb.at[c, some], s9.at[m - 1], v9.at[m - 1], at_col(col_peer(m), k)) for m in flips]
        for copy in copies:
            copy.wait()
        total = gb[0, some]
        for to in range(1, cols):
            total = total + gb[to, some]
        there = slice(first, first + count)
        gf[r, there] = total
        send(gf.at[r, there], gf.at[r, there], sf.at[0, 0], vf.at[k, 0], partner)
        for s in range(1, groups):
            for n, core in enumerate((k, other)):
                send(gf.at[r, there], gf.at[r, there], sf.at[s, n], vf.at[k, s], at_row(row_peer(s), core))
        for copy in image_copies((1,) if first == 0 else (0, 1)):
            copy.start()

    @pl.when(k == 0)
    def _():
        gram(0, 1)

    @pl.when(k == 1)
    def _():
        pair.wait_recv()
        gram(1, 2)

    def gathered(first, count):
        there = slice(first, first + count)
        source = min(first, 1)

        @pl.when(k != source)
        def _():
            arrive(gf.at[r, there], vf.at[source, 0])

        for s in range(1, groups):
            arrive(gf.at[lax.rem(r + groups - s, groups), there], vf.at[source, s])

    def whole(n):
        return jnp.concatenate([gf[g, n] for g in range(groups)], axis=0)

    gathered(0, 1)
    s0_ref[...] = whole(0)
    eliminate(s0_ref, w0_ref)
    gathered(1, 2)
    upper = exact(w0_ref[...], whole(1), 1, 0)
    s1_ref[...] = whole(2) - exact(upper, upper, 0, 0)
    cross = exact(upper, w0_ref[...], 0, 0)
    eliminate(s1_ref, w1_ref)
    row = lax.broadcasted_iota(jnp.int32, (width, width), 0)
    col = lax.broadcasted_iota(jnp.int32, (width, width), 1)
    zero = jnp.zeros((width, width), F32)
    low, high = slice(0, width), slice(width, 2 * width)
    factor_ref[low, low] = jnp.where(row <= col, s0_ref[...], 0.0) / root
    factor_ref[low, high] = upper / root
    factor_ref[high, low] = zero
    factor_ref[high, high] = jnp.where(row <= col, s1_ref[...], 0.0) / root
    w_ref[low, low] = w0_ref[...]
    w_ref[low, high] = zero
    w_ref[high, low] = -exact(w1_ref[...], cross, 1, 0)
    w_ref[high, high] = w1_ref[...]

    @pl.when(k == 0)
    def _():
        pair.wait_recv()

    im[c, k] = x[k, k]
    im[c, other] = x[other, k]
    for j in range(2):
        for m in flips:
            arrive(im.at[col_peer(m), j], v8.at[j, m - 1])
    columns = inverse_ref.shape[0]
    inverse_ref[...] = w_ref[pl.ds(pl.multiple_of(c * columns, columns), columns), :]
    for copy in first_sums[1]:
        copy.wait_send()
    for copy in sends:
        copy.wait_send()
    copy_of(sg.at[0], sk.at[k, c], pair_s.at[1], pair_v.at[1], partner).wait_send()
    pair.wait_send()
    for copy in image_copies():
        copy.wait_send()

    def sent(first, count):
        there = slice(first, first + count)
        copy_of(gf.at[r, there], gf.at[r, there], sf.at[0, 0], vf.at[k, 0], partner).wait_send()
        for s in range(1, groups):
            for n, core in enumerate((k, other)):
                copy_of(gf.at[r, there], gf.at[r, there], sf.at[s, n], vf.at[k, s], at_row(row_peer(s), core)).wait_send()

    @pl.when(k == 0)
    def _():
        sent(0, 1)

    @pl.when(k == 1)
    def _():
        sent(1, 2)


def basis_kernel(root, inverse_ref, im, factor_ref, basis_ref, out_ref):
    out_ref[...] = factor_ref[...]
    cols, parts, part, width = im.shape
    rows = [jnp.concatenate([im[to, n] for to in range(cols)], axis=0) for n in range(parts)]
    image = jnp.concatenate(rows, axis=1)
    basis_ref[...] = exact(inverse_ref[...], image, 1, 1) * root


def power_step(operator, test_matrix, sizes, ratio, root):
    outer, inner, cols = sizes
    rows, depth = operator.shape
    rank = test_matrix.shape[1]
    half = rank // 2
    groups = outer * inner // 2
    part = rows // cols
    lanes = half // groups
    dma = pltpu.SemaphoreType.DMA
    vmem = pltpu.VMEM
    blocks = (2, cols - 1, part, half)
    span = depth // SPANS
    scratch = [
        vmem((2, rows, depth), BF16),
        vmem((depth, rank), BF16),
        vmem((2, rows, half), F32),
        vmem((2, rows, half), BF16),
        vmem(blocks, F32),
        vmem(blocks, BF16),
        vmem((2, part, half), BF16),
        vmem((2, cols, part, half), BF16),
        vmem((SPANS, groups, lanes, span), F32),
        vmem((SPANS, groups, lanes, span), BF16),
        vmem((SPANS, groups - 1, lanes, span), BF16),
        vmem((SPANS, groups, lanes, span), BF16),
        vmem((2, rows, half), F32),
        vmem((2, rows, half), BF16),
        vmem(blocks, F32),
        vmem(blocks, BF16),
        vmem((2, 2, part, half), F32),
        vmem((groups, 2, lanes, half), F32),
        vmem((groups - 1, 2, lanes, half), F32),
        vmem((cols, 2, lanes, half), F32),
        vmem((groups, 3, lanes, half), F32),
        vmem((half, half), F32),
        vmem((half, half), F32),
        vmem((half, half), F32),
        vmem((half, half), F32),
        vmem((rank, rank), F32),
        dma((3,)),
        dma((3,)), dma((3,)),
    ]
    across, along = (2, cols - 1), (SPANS, groups - 1)
    for shape in (across, across, along, along, across):
        scratch += [dma(shape), dma(shape)]
    scratch += [dma((groups - 1,)), dma((groups - 1,))]
    scratch += [dma((cols - 1, 2)), dma((2, cols - 1))]
    scratch += [dma((cols - 1,)), dma((cols - 1,))]
    scratch += [dma((groups, 2)), dma((2, groups))]
    whole = pl.BlockSpec(memory_space=pltpu.VMEM)
    inverse, image, factor = pl.pallas_call(
        functools.partial(power_kernel, sizes, ratio, root),
        out_shape=(
            jax.ShapeDtypeStruct((rank // cols, rank), F32),
            jax.ShapeDtypeStruct((cols, 2, part, half), F32),
            jax.ShapeDtypeStruct((rank, rank), F32),
        ),
        in_specs=[pl.BlockSpec(memory_space=pl.ANY)] * 2,
        out_specs=(whole,) * 3,
        scratch_shapes=scratch,
        compiler_params=pltpu.CompilerParams(
            collective_id=0, has_side_effects=True, vmem_limit_bytes=53 << 20
        ),
        name="power_step",
    )(operator, test_matrix)
    return pl.pallas_call(
        functools.partial(basis_kernel, root),
        out_shape=(
            jax.ShapeDtypeStruct((rank // cols, rows), F32),
            jax.ShapeDtypeStruct((rank, rank), F32),
        ),
        in_specs=[whole] * 3,
        out_specs=(whole,) * 2,
        compiler_params=pltpu.CompilerParams(vmem_limit_bytes=8 << 20),
        name="basis",
    )(inverse, image, factor)


def shards(operator, test_matrix):
    sizes = tuple(lax.axis_size(name) for name in ("outer", "inner", "col"))
    row_groups = sizes[0] * sizes[1]
    col_groups = sizes[2]
    total_rows = operator.shape[0] * row_groups
    total_cols = operator.shape[1] * col_groups
    root = float(total_rows) ** 0.5
    basis, factor = power_step(operator, test_matrix, sizes, total_cols / total_rows, root)
    return (basis.T, factor)


def solution(mesh):
    placed = (P(("outer", "inner"), "col"), P("col", None))
    return jax.shard_map(
        shards,
        mesh=mesh,
        in_specs=placed,
        out_specs=(P(("outer", "inner"), "col"), P()),
        check_vma=False,
    )
```

```python
import functools

import jax
import jax.numpy as jnp
from jax import lax
from jax.experimental import pallas as pl
from jax.experimental.pallas import tpu as pltpu
from jax.sharding import PartitionSpec as P

F32 = jnp.float32
BF16 = jnp.bfloat16
MESH = pl.DeviceIdType.MESH
HIGHEST = lax.Precision.HIGHEST
SPANS = 4
BLOCK = 32


def wide_sketch(half, flip):
    return flip == 1


def wide_image(flip):
    return False


def split(value):
    high = value.astype(BF16)
    rest = value - high.astype(F32)
    middle = rest.astype(BF16)
    low = (rest - middle.astype(F32)).astype(BF16)
    return high, middle, low


def eliminate(s_ref, w_ref):
    size = s_ref.shape[0]
    row = lax.broadcasted_iota(jnp.int32, (size, size), 0)
    col = lax.broadcasted_iota(jnp.int32, (size, size), 1)
    w_ref[...] = jnp.where(row == col, jnp.float32(1), jnp.float32(0))
    sub = lax.broadcasted_iota(jnp.int32, (8, 128), 0)
    wide = 128
    for start in range(0, size, BLOCK):
        rows = BLOCK // 8
        tiles = [(s_ref, t) for t in range(start // wide, size // wide)]
        tiles += [(w_ref, t) for t in range(0, start // wide + 1)]
        q = [[ref[start + 8 * g:start + 8 * g + 8, t * wide:(t + 1) * wide] for ref, t in tiles]
             for g in range(rows)]
        for p in range(rows):
            first = (start + 8 * p) % wide
            cs = [[jnp.broadcast_to(q[g][0][:, first + n:first + n + 1], (8, wide)) for n in range(8)]
                  for g in range(p, rows)]
            pivots = jnp.zeros((8, wide), F32)
            for n in range(8):
                pivot = jnp.broadcast_to(cs[0][n][n:n + 1], (8, wide))
                pivots = jnp.where(sub == n, pivot, pivots)
                inverse = 1.0 / pivot
                heads = {m: jnp.broadcast_to(cs[0][m][n:n + 1], (8, wide)) * inverse for m in range(n + 1, 8)}
                bodies = [jnp.broadcast_to(tile[n:n + 1], (8, wide)) * inverse for tile in q[p]]
                for g in range(p, rows):
                    weight = cs[g - p][n]
                    if g == p:
                        weight = jnp.where(sub > n, weight, 0.0)
                    for m in range(n + 1, 8):
                        cs[g - p][m] = cs[g - p][m] - weight * heads[m]
                    q[g] = [tile - weight * body for tile, body in zip(q[g], bodies)]
            scale = lax.rsqrt(pivots)
            q[p] = [tile * scale for tile in q[p]]
        for g in range(rows):
            for (ref, t), tile in zip(tiles, q[g]):
                ref[start + 8 * g:start + 8 * g + 8, t * wide:(t + 1) * wide] = tile
        done = start + BLOCK
        if done < size:
            block = jnp.concatenate([jnp.concatenate(q[g], axis=1) for g in range(rows)], axis=0)
            h, m, l = split(block)
            count = size // wide - start // wide
            base = (start // wide) * wide
            take = slice(done - base, count * wide) if (done - base) % wide == 0 else slice(0, count * wide)
            skip = done - base - (take.start or 0)
            left = jnp.concatenate([h, h, m, m, h, l], axis=0)[:, take]
            right = jnp.concatenate([h, m, h, m, l, h], axis=0)
            update = lax.dot_general(left, right, (((0,), (0,)), ((), ())), preferred_element_type=F32)[skip:]
            for at, (ref, t) in enumerate(tiles):
                lanes = slice(t * wide, (t + 1) * wide)
                ref[done:, lanes] = ref[done:, lanes] - update[:, at * wide:(at + 1) * wide]


def exact(left, right, left_dim, right_dim):
    return lax.dot_general(left, right, (((left_dim,), (right_dim,)), ((), ())),
                           precision=HIGHEST, preferred_element_type=F32)


def power_kernel(
    sizes, ratio, root, a_hbm, om_hbm, inverse_ref, im, factor_ref,
    a, om, p1, w1, r1, n1, sg, sk, p2, w2, r2, nt, p3, w3, r3, n3, x, gp, ra, gb, gf, s0_ref, s1_ref, w0_ref, w1_ref,
    load_sem, pair_s, pair_v, s1, v1, s2, v2, s3, v3, s4, v4, s5, v5, s7, v7, s8, v8, s9, v9, sf, vf,
):
    outer, inner, cols = sizes
    chips = inner // 2
    groups = outer * chips
    o, i, c = lax.axis_index("outer"), lax.axis_index("inner"), lax.axis_index("col")
    k = lax.rem(i, 2)
    other = 1 - k
    chip = lax.div(i, 2)
    r = o * chips + chip
    partner = (o, chip * 2 + other, c)
    flips = (2, 3, 1)

    def col_peer(m):
        return jnp.bitwise_xor(c, m)

    def row_peer(s):
        return lax.rem(r + s, groups)

    def at_col(to, core):
        return (o, chip * 2 + core, to)

    def at_row(to, core):
        return (lax.div(to, chips), lax.rem(to, chips) * 2 + core, c)

    def copy_of(src, dst, ss, rs, to):
        return pltpu.make_async_remote_copy(
            src_ref=src, dst_ref=dst, send_sem=ss, recv_sem=rs, device_id=to, device_id_type=MESH
        )

    def send(src, dst, ss, rs, to):
        copy = copy_of(src, dst, ss, rs, to)
        copy.start()
        return copy

    def arrive(dst, rs):
        copy_of(dst, dst, rs, rs, partner).wait_recv()

    width = om.shape[1] // 2

    def lanes_of(h):
        return slice(h * width, (h + 1) * width)

    load_a = pltpu.make_async_copy(a_hbm, a.at[k], load_sem.at[0])
    load_a.start()
    load_om = [pltpu.make_async_copy(om_hbm.at[:, lanes_of(h)], om.at[:, lanes_of(h)], load_sem.at[1 + h]) for h in range(2)]
    for load in load_om:
        load.start()

    barrier = pltpu.get_barrier_semaphore()
    peers = [partner]
    for m in flips:
        peers += [at_col(col_peer(m), k), at_col(col_peer(m), other)]
    for s in range(1, groups):
        peers += [at_row(row_peer(s), k), at_row(row_peer(s), other)]
    for to in peers:
        pl.semaphore_signal(barrier, inc=1, device_id=to, device_id_type=MESH)
    load_a.wait()

    part = p1.shape[1] // cols
    own = pl.ds(pl.multiple_of(c * part, part), part)

    def rows_of(to):
        return pl.ds(pl.multiple_of(to * part, part), part)

    sends = []
    sums = []
    for h in range(2):
        load_om[h].wait()
        p1[h] = jnp.dot(a[k], om[:, lanes_of(h)], preferred_element_type=F32)
        if not all(wide_sketch(h, m) for m in flips):
            w1[h] = p1[h].astype(BF16)
        if h == 0:
            pl.semaphore_wait(barrier, len(peers))
        copies = []
        for n, m in enumerate(flips):
            if h == 1:
                sums[0][n].wait_send()
            to = col_peer(m)
            src, dst = (p1, r1) if wide_sketch(h, m) else (w1, n1)
            copies.append(send(src.at[h, rows_of(to)], dst.at[h, m - 1], s1.at[h, m - 1], v1.at[h, m - 1], at_col(to, k)))
        sums.append(copies)
        if h == 0:
            swap = send(a_hbm, a.at[k], pair_s.at[0], pair_v.at[0], partner)
    first_sums = sums
    for h in range(2):
        for copy in sums[h]:
            copy.wait_recv()
        total = p1[h, own]
        for m in flips:
            total = total + (r1[h, m - 1] if wide_sketch(h, m) else n1[h, m - 1].astype(F32))
        sg[h] = total.astype(BF16)
        for m in flips:
            sends.append(send(sg.at[h], sk.at[k, c], s2.at[h, m - 1], v2.at[k, m - 1], at_col(col_peer(m), h)))

        @pl.when(k == h)
        def _():
            sk[k, c] = sg[h]

        @pl.when(k != h)
        def _():
            send(sg.at[h], sk.at[k, c], pair_s.at[1], pair_v.at[1], partner)

    swap.wait()
    arrive(sk.at[other, c], pair_v.at[1])
    turned = []
    for j in range(2):
        for m in flips:
            arrive(sk.at[j, col_peer(m)], v2.at[j, m - 1])
        turned.append(jnp.concatenate([sk[j, to] for to in range(cols)], axis=0).astype(F32).T.astype(BF16))
    lanes = p2.shape[2]
    depth = p2.shape[3]
    sums = []
    for span in range(SPANS):
        at = slice(span * depth, (span + 1) * depth)
        normal = None
        for j in range(2):
            term = jnp.dot(turned[j], a[j, :, at], preferred_element_type=F32)
            normal = term if normal is None else normal + term
        for g in range(groups):
            p2[span, g] = normal[g * lanes:(g + 1) * lanes]
            w2[span, g] = normal[g * lanes:(g + 1) * lanes].astype(BF16)
        copies = []
        for s in range(1, groups):
            to = row_peer(s)
            copies.append(send(w2.at[span, to], r2.at[span, s - 1], s3.at[span, s - 1], v3.at[span, s - 1], at_row(to, k)))
        sums.append(copies)
    wholes = []
    for span in range(SPANS):
        for copy in sums[span]:
            copy.wait()
        total = p2[span, r]
        for s in range(1, groups):
            total = total + r2[span, s - 1].astype(F32)
        nt[span, r] = (total * ratio).astype(BF16)
        copies = []
        for s in range(1, groups):
            copies.append(send(nt.at[span, r], nt.at[span, r], s4.at[span, s - 1], v4.at[span, s - 1], at_row(row_peer(s), k)))
        wholes.append(copies)

    spans = []
    sums = []
    for span in range(SPANS):
        for copy in wholes[span]:
            copy.wait()
        if lanes % 16 == 0:
            spans.append(nt[span].reshape(groups * lanes, depth))
        else:
            spans.append(jnp.concatenate([nt[span, g].astype(F32) for g in range(groups)], axis=0).astype(BF16))
        for block in range(2):
            term = lax.dot_general(a[block, :, span * depth:(span + 1) * depth], spans[span],
                                   (((1,), (1,)), ((), ())), preferred_element_type=F32)
            if span > 0:
                term = p3[block] + term
            p3[block] = term
            if span < SPANS - 1:
                continue
            w3[block] = term.astype(BF16)
            copies = []
            for m in flips:
                to = col_peer(m)
                src, dst = (p3, r3) if wide_image(m) else (w3, n3)
                copies.append(send(src.at[block, rows_of(to)], dst.at[block, m - 1],
                                   s5.at[block, m - 1], v5.at[block, m - 1], at_col(to, k)))
            sums.append(copies)
    for block in range(2):
        for copy in sums[block]:
            copy.wait()
        total = p3[block, own]
        for m in flips:
            total = total + (r3[block, m - 1] if wide_image(m) else n3[block, m - 1].astype(F32))
        x[k, block] = total
    pair = send(x.at[k], x.at[k], pair_s.at[2], pair_v.at[2], partner)

    def image_copies(turns=(0, 1)):
        return [
            copy_of(x.at[k, core], im.at[c, k], s8.at[m - 1, n], v8.at[k, m - 1], at_col(col_peer(m), core))
            for m in flips for n, core in enumerate((k, other)) if n in turns
        ]

    piece = gp.shape[2]

    def gram(first, count):
        mine = x[k].reshape(2 * part, width)
        for n in range(count):
            full = exact(x[n].reshape(2 * part, width), mine, 0, 0)
            for to in range(groups):
                gp[to, n] = full[to * piece:(to + 1) * piece]
        some = slice(0, count)
        copies = []
        for s in range(1, groups):
            to = row_peer(s)
            copies.append(send(gp.at[to, some], ra.at[s - 1, some], s7.at[s - 1], v7.at[s - 1], at_row(to, k)))
        if first == 0:
            for copy in image_copies((0,)):
                copy.start()
        for copy in copies:
            copy.wait()
        total = gp[r, some]
        for s in range(1, groups):
            total = total + ra[s - 1, some]
        gb[c, some] = total
        copies = [send(gb.at[c, some], gb.at[c, some], s9.at[m - 1], v9.at[m - 1], at_col(col_peer(m), k)) for m in flips]
        for copy in copies:
            copy.wait()
        total = gb[0, some]
        for to in range(1, cols):
            total = total + gb[to, some]
        there = slice(first, first + count)
        gf[r, there] = total
        send(gf.at[r, there], gf.at[r, there], sf.at[0, 0], vf.at[k, 0], partner)
        for s in range(1, groups):
            for n, core in enumerate((k, other)):
                send(gf.at[r, there], gf.at[r, there], sf.at[s, n], vf.at[k, s], at_row(row_peer(s), core))
        for copy in image_copies((1,) if first == 0 else (0, 1)):
            copy.start()

    @pl.when(k == 0)
    def _():
        gram(0, 1)

    @pl.when(k == 1)
    def _():
        pair.wait_recv()
        gram(1, 2)

    def gathered(first, count):
        there = slice(first, first + count)
        source = min(first, 1)

        @pl.when(k != source)
        def _():
            arrive(gf.at[r, there], vf.at[source, 0])

        for s in range(1, groups):
            arrive(gf.at[lax.rem(r + groups - s, groups), there], vf.at[source, s])

    def whole(n):
        return jnp.concatenate([gf[g, n] for g in range(groups)], axis=0)

    gathered(0, 1)
    s0_ref[...] = whole(0)
    eliminate(s0_ref, w0_ref)
    gathered(1, 2)
    upper = exact(w0_ref[...], whole(1), 1, 0)
    s1_ref[...] = whole(2) - exact(upper, upper, 0, 0)
    cross = exact(upper, w0_ref[...], 0, 0)
    row = lax.broadcasted_iota(jnp.int32, (width, width), 0)
    col = lax.broadcasted_iota(jnp.int32, (width, width), 1)
    low, high = slice(0, width), slice(width, 2 * width)
    factor_ref[low, low] = jnp.where(row <= col, s0_ref[...], 0.0) / root
    factor_ref[low, high] = upper / root
    factor_ref[high, low] = jnp.zeros((width, width), F32)
    eliminate(s1_ref, w1_ref)
    factor_ref[high, high] = jnp.where(row <= col, s1_ref[...], 0.0) / root
    columns = inverse_ref.shape[0]
    first = c * columns
    mine = pl.ds(pl.multiple_of(lax.rem(first, width), columns), columns)
    last = w1_ref[mine, :]
    before = first < width
    inverse_ref[:, low] = jnp.where(before, w0_ref[mine, :], -exact(last, cross, 1, 0))
    inverse_ref[:, high] = jnp.where(before, 0.0, last)

    @pl.when(k == 0)
    def _():
        pair.wait_recv()

    im[c, k] = x[k, k]
    im[c, other] = x[other, k]
    for j in range(2):
        for m in flips:
            arrive(im.at[col_peer(m), j], v8.at[j, m - 1])
    for copy in first_sums[1]:
        copy.wait_send()
    for copy in sends:
        copy.wait_send()
    copy_of(sg.at[0], sk.at[k, c], pair_s.at[1], pair_v.at[1], partner).wait_send()
    pair.wait_send()
    for copy in image_copies():
        copy.wait_send()

    def sent(first, count):
        there = slice(first, first + count)
        copy_of(gf.at[r, there], gf.at[r, there], sf.at[0, 0], vf.at[k, 0], partner).wait_send()
        for s in range(1, groups):
            for n, core in enumerate((k, other)):
                copy_of(gf.at[r, there], gf.at[r, there], sf.at[s, n], vf.at[k, s], at_row(row_peer(s), core)).wait_send()

    @pl.when(k == 0)
    def _():
        sent(0, 1)

    @pl.when(k == 1)
    def _():
        sent(1, 2)


def basis_kernel(root, inverse_ref, im, factor_ref, basis_ref, out_ref):
    out_ref[...] = factor_ref[...]
    cols, parts, part, width = im.shape
    rows = [jnp.concatenate([im[to, n] for to in range(cols)], axis=0) for n in range(parts)]
    image = jnp.concatenate(rows, axis=1)
    size = inverse_ref.shape[0]
    left, left_rest, _ = split(inverse_ref[...])
    right, right_rest, _ = split(image)
    dims = (((1,), (1,)), ((), ()))
    both = lax.dot_general(jnp.concatenate([left, left_rest], axis=0), right, dims, preferred_element_type=F32)
    rest = lax.dot_general(left, right_rest, dims, preferred_element_type=F32)
    basis_ref[...] = (both[:size] + (both[size:] + rest)) * root


def power_step(operator, test_matrix, sizes, ratio, root):
    outer, inner, cols = sizes
    rows, depth = operator.shape
    rank = test_matrix.shape[1]
    half = rank // 2
    groups = outer * inner // 2
    part = rows // cols
    lanes = half // groups
    dma = pltpu.SemaphoreType.DMA
    vmem = pltpu.VMEM
    blocks = (2, cols - 1, part, half)
    span = depth // SPANS
    scratch = [
        vmem((2, rows, depth), BF16),
        vmem((depth, rank), BF16),
        vmem((2, rows, half), F32),
        vmem((2, rows, half), BF16),
        vmem(blocks, F32),
        vmem(blocks, BF16),
        vmem((2, part, half), BF16),
        vmem((2, cols, part, half), BF16),
        vmem((SPANS, groups, lanes, span), F32),
        vmem((SPANS, groups, lanes, span), BF16),
        vmem((SPANS, groups - 1, lanes, span), BF16),
        vmem((SPANS, groups, lanes, span), BF16),
        vmem((2, rows, half), F32),
        vmem((2, rows, half), BF16),
        vmem(blocks, F32),
        vmem(blocks, BF16),
        vmem((2, 2, part, half), F32),
        vmem((groups, 2, lanes, half), F32),
        vmem((groups - 1, 2, lanes, half), F32),
        vmem((cols, 2, lanes, half), F32),
        vmem((groups, 3, lanes, half), F32),
        vmem((half, half), F32),
        vmem((half, half), F32),
        vmem((half, half), F32),
        vmem((half, half), F32),
        dma((3,)),
        dma((3,)), dma((3,)),
    ]
    across, along = (2, cols - 1), (SPANS, groups - 1)
    for shape in (across, across, along, along, across):
        scratch += [dma(shape), dma(shape)]
    scratch += [dma((groups - 1,)), dma((groups - 1,))]
    scratch += [dma((cols - 1, 2)), dma((2, cols - 1))]
    scratch += [dma((cols - 1,)), dma((cols - 1,))]
    scratch += [dma((groups, 2)), dma((2, groups))]
    whole = pl.BlockSpec(memory_space=pltpu.VMEM)
    inverse, image, factor = pl.pallas_call(
        functools.partial(power_kernel, sizes, ratio, root),
        out_shape=(
            jax.ShapeDtypeStruct((rank // cols, rank), F32),
            jax.ShapeDtypeStruct((cols, 2, part, half), F32),
            jax.ShapeDtypeStruct((rank, rank), F32),
        ),
        in_specs=[pl.BlockSpec(memory_space=pl.ANY)] * 2,
        out_specs=(whole,) * 3,
        scratch_shapes=scratch,
        compiler_params=pltpu.CompilerParams(
            collective_id=0, has_side_effects=True, vmem_limit_bytes=53 << 20
        ),
        name="power_step",
    )(operator, test_matrix)
    return pl.pallas_call(
        functools.partial(basis_kernel, root),
        out_shape=(
            jax.ShapeDtypeStruct((rank // cols, rows), F32),
            jax.ShapeDtypeStruct((rank, rank), F32),
        ),
        in_specs=[whole] * 3,
        out_specs=(whole,) * 2,
        compiler_params=pltpu.CompilerParams(vmem_limit_bytes=8 << 20),
        name="basis",
    )(inverse, image, factor)


def shards(operator, test_matrix):
    sizes = tuple(lax.axis_size(name) for name in ("outer", "inner", "col"))
    row_groups = sizes[0] * sizes[1]
    col_groups = sizes[2]
    total_rows = operator.shape[0] * row_groups
    total_cols = operator.shape[1] * col_groups
    root = float(total_rows) ** 0.5
    basis, factor = power_step(operator, test_matrix, sizes, total_cols / total_rows, root)
    return (basis.T, factor)


def solution(mesh):
    placed = (P(("outer", "inner"), "col"), P("col", None))
    return jax.shard_map(
        shards,
        mesh=mesh,
        in_specs=placed,
        out_specs=(P(("outer", "inner"), "col"), P()),
        check_vma=False,
    )
```

```python
import functools

import jax
import jax.numpy as jnp
from jax import lax
from jax.experimental import pallas as pl
from jax.experimental.pallas import tpu as pltpu
from jax.sharding import PartitionSpec as P

F32 = jnp.float32
BF16 = jnp.bfloat16
MESH = pl.DeviceIdType.MESH
HIGHEST = lax.Precision.HIGHEST
SPANS = 4
LOADS = 4
BLOCK = 32


def wide_sketch(half, flip):
    return flip == 1


def wide_image(flip):
    return False


def split(value):
    high = value.astype(BF16)
    rest = value - high.astype(F32)
    middle = rest.astype(BF16)
    low = (rest - middle.astype(F32)).astype(BF16)
    return high, middle, low


def eliminate(s_ref, w_ref):
    size = s_ref.shape[0]
    row = lax.broadcasted_iota(jnp.int32, (size, size), 0)
    col = lax.broadcasted_iota(jnp.int32, (size, size), 1)
    w_ref[...] = jnp.where(row == col, jnp.float32(1), jnp.float32(0))
    sub = lax.broadcasted_iota(jnp.int32, (8, 128), 0)
    wide = 128
    for start in range(0, size, BLOCK):
        rows = BLOCK // 8
        tiles = [(s_ref, t) for t in range(start // wide, size // wide)]
        tiles += [(w_ref, t) for t in range(0, start // wide + 1)]
        q = [[ref[start + 8 * g:start + 8 * g + 8, t * wide:(t + 1) * wide] for ref, t in tiles]
             for g in range(rows)]
        for p in range(rows):
            first = (start + 8 * p) % wide
            cs = [[jnp.broadcast_to(q[g][0][:, first + n:first + n + 1], (8, wide)) for n in range(8)]
                  for g in range(p, rows)]
            pivots = jnp.zeros((8, wide), F32)
            for n in range(8):
                pivot = jnp.broadcast_to(cs[0][n][n:n + 1], (8, wide))
                pivots = jnp.where(sub == n, pivot, pivots)
                inverse = 1.0 / pivot
                heads = {m: jnp.broadcast_to(cs[0][m][n:n + 1], (8, wide)) * inverse for m in range(n + 1, 8)}
                bodies = [jnp.broadcast_to(tile[n:n + 1], (8, wide)) * inverse for tile in q[p]]
                for g in range(p, rows):
                    weight = cs[g - p][n]
                    if g == p:
                        weight = jnp.where(sub > n, weight, 0.0)
                    for m in range(n + 1, 8):
                        cs[g - p][m] = cs[g - p][m] - weight * heads[m]
                    q[g] = [tile - weight * body for tile, body in zip(q[g], bodies)]
            scale = lax.rsqrt(pivots)
            q[p] = [tile * scale for tile in q[p]]
        for g in range(rows):
            for (ref, t), tile in zip(tiles, q[g]):
                ref[start + 8 * g:start + 8 * g + 8, t * wide:(t + 1) * wide] = tile
        done = start + BLOCK
        if done < size:
            block = jnp.concatenate([jnp.concatenate(q[g], axis=1) for g in range(rows)], axis=0)
            h, m, l = split(block)
            count = size // wide - start // wide
            base = (start // wide) * wide
            take = slice(done - base, count * wide) if (done - base) % wide == 0 else slice(0, count * wide)
            skip = done - base - (take.start or 0)
            left = jnp.concatenate([h, h, m, m, h, l], axis=0)[:, take]
            right = jnp.concatenate([h, m, h, m, l, h], axis=0)
            update = lax.dot_general(left, right, (((0,), (0,)), ((), ())), preferred_element_type=F32)[skip:]
            for at, (ref, t) in enumerate(tiles):
                lanes = slice(t * wide, (t + 1) * wide)
                ref[done:, lanes] = ref[done:, lanes] - update[:, at * wide:(at + 1) * wide]


def exact(left, right, left_dim, right_dim):
    return lax.dot_general(left, right, (((left_dim,), (right_dim,)), ((), ())),
                           precision=HIGHEST, preferred_element_type=F32)


def power_kernel(
    sizes, ratio, root, a_hbm, om_hbm, inverse_ref, im, factor_ref,
    a, om, p1, w1, r1, n1, sg, sk, p2, w2, r2, nt, p3, w3, r3, n3, x, gp, ra, gb, gf, s0_ref, s1_ref, w0_ref, w1_ref,
    load_sem, pair_s, pair_v, s1, v1, s2, v2, s3, v3, s4, v4, s5, v5, s7, v7, s8, v8, s9, v9, sf, vf,
):
    outer, inner, cols = sizes
    chips = inner // 2
    groups = outer * chips
    o, i, c = lax.axis_index("outer"), lax.axis_index("inner"), lax.axis_index("col")
    k = lax.rem(i, 2)
    other = 1 - k
    chip = lax.div(i, 2)
    r = o * chips + chip
    partner = (o, chip * 2 + other, c)
    flips = (2, 3, 1)

    def col_peer(m):
        return jnp.bitwise_xor(c, m)

    def row_peer(s):
        return lax.rem(r + s, groups)

    def at_col(to, core):
        return (o, chip * 2 + core, to)

    def at_row(to, core):
        return (lax.div(to, chips), lax.rem(to, chips) * 2 + core, c)

    def copy_of(src, dst, ss, rs, to):
        return pltpu.make_async_remote_copy(
            src_ref=src, dst_ref=dst, send_sem=ss, recv_sem=rs, device_id=to, device_id_type=MESH
        )

    def send(src, dst, ss, rs, to):
        copy = copy_of(src, dst, ss, rs, to)
        copy.start()
        return copy

    def arrive(dst, rs):
        copy_of(dst, dst, rs, rs, partner).wait_recv()

    width = om.shape[1] // 2

    def lanes_of(h):
        return slice(h * width, (h + 1) * width)

    depths = [slice(n * (om.shape[0] // LOADS), (n + 1) * (om.shape[0] // LOADS)) for n in range(LOADS)]
    loads = []
    for n, at in enumerate(depths):
        loads.append([
            pltpu.make_async_copy(a_hbm.at[:, at], a.at[k, :, at], load_sem.at[n, 0]),
            pltpu.make_async_copy(om_hbm.at[at], om.at[at], load_sem.at[n, 1]),
        ])
        for load in loads[n]:
            load.start()

    barrier = pltpu.get_barrier_semaphore()
    peers = [partner]
    for m in flips:
        peers += [at_col(col_peer(m), k), at_col(col_peer(m), other)]
    for s in range(1, groups):
        peers += [at_row(row_peer(s), k), at_row(row_peer(s), other)]
    for to in peers:
        pl.semaphore_signal(barrier, inc=1, device_id=to, device_id_type=MESH)

    part = p1.shape[1] // cols
    own = pl.ds(pl.multiple_of(c * part, part), part)

    def rows_of(to):
        return pl.ds(pl.multiple_of(to * part, part), part)

    sends = []
    sums = []
    for h in range(2):
        product = None
        for n, at in enumerate(depths):
            if h == 0:
                for load in loads[n]:
                    load.wait()
            term = jnp.dot(a[k, :, at], om[at, lanes_of(h)], preferred_element_type=F32)
            product = term if product is None else product + term
        p1[h] = product
        if not all(wide_sketch(h, m) for m in flips):
            w1[h] = p1[h].astype(BF16)
        if h == 0:
            pl.semaphore_wait(barrier, len(peers))
        copies = []
        for n, m in enumerate(flips):
            to = col_peer(m)
            src, dst = (p1, r1) if wide_sketch(h, m) else (w1, n1)
            copies.append(send(src.at[h, rows_of(to)], dst.at[h, m - 1], s1.at[h, m - 1], v1.at[h, m - 1], at_col(to, k)))
        sums.append(copies)
        if h == 0:
            swap = send(a_hbm, a.at[k], pair_s.at[0], pair_v.at[0], partner)
    first_sums = sums
    for h in range(2):
        for copy in sums[h]:
            copy.wait_recv()
        total = p1[h, own]
        for m in flips:
            total = total + (r1[h, m - 1] if wide_sketch(h, m) else n1[h, m - 1].astype(F32))
        sg[h] = total.astype(BF16)
        for m in flips:
            sends.append(send(sg.at[h], sk.at[k, c], s2.at[h, m - 1], v2.at[k, m - 1], at_col(col_peer(m), h)))

        @pl.when(k == h)
        def _():
            sk[k, c] = sg[h]

        @pl.when(k != h)
        def _():
            send(sg.at[h], sk.at[k, c], pair_s.at[1], pair_v.at[1], partner)

    swap.wait()
    arrive(sk.at[other, c], pair_v.at[1])
    turned = []
    for j in range(2):
        for m in flips:
            arrive(sk.at[j, col_peer(m)], v2.at[j, m - 1])
        turned.append(jnp.concatenate([sk[j, to] for to in range(cols)], axis=0).astype(F32).T.astype(BF16))
    lanes = p2.shape[2]
    depth = p2.shape[3]
    sums = []
    for span in range(SPANS):
        at = slice(span * depth, (span + 1) * depth)
        normal = None
        for j in range(2):
            term = jnp.dot(turned[j], a[j, :, at], preferred_element_type=F32)
            normal = term if normal is None else normal + term
        for g in range(groups):
            p2[span, g] = normal[g * lanes:(g + 1) * lanes]
            w2[span, g] = normal[g * lanes:(g + 1) * lanes].astype(BF16)
        copies = []
        for s in range(1, groups):
            to = row_peer(s)
            copies.append(send(w2.at[span, to], r2.at[span, s - 1], s3.at[span, s - 1], v3.at[span, s - 1], at_row(to, k)))
        sums.append(copies)
    wholes = []
    for span in range(SPANS):
        for copy in sums[span]:
            copy.wait()
        total = p2[span, r]
        for s in range(1, groups):
            total = total + r2[span, s - 1].astype(F32)
        nt[span, r] = (total * ratio).astype(BF16)
        copies = []
        for s in range(1, groups):
            copies.append(send(nt.at[span, r], nt.at[span, r], s4.at[span, s - 1], v4.at[span, s - 1], at_row(row_peer(s), k)))
        wholes.append(copies)

    spans = []
    sums = []
    for span in range(SPANS):
        for copy in wholes[span]:
            copy.wait()
        if lanes % 16 == 0:
            spans.append(nt[span].reshape(groups * lanes, depth))
        else:
            spans.append(jnp.concatenate([nt[span, g].astype(F32) for g in range(groups)], axis=0).astype(BF16))
        for block in range(2):
            term = lax.dot_general(a[block, :, span * depth:(span + 1) * depth], spans[span],
                                   (((1,), (1,)), ((), ())), preferred_element_type=F32)
            if span > 0:
                term = p3[block] + term
            p3[block] = term
            if span < SPANS - 1:
                continue
            w3[block] = term.astype(BF16)
            copies = []
            for m in flips:
                to = col_peer(m)
                src, dst = (p3, r3) if wide_image(m) else (w3, n3)
                copies.append(send(src.at[block, rows_of(to)], dst.at[block, m - 1],
                                   s5.at[block, m - 1], v5.at[block, m - 1], at_col(to, k)))
            sums.append(copies)
    for block in range(2):
        for copy in sums[block]:
            copy.wait()
        total = p3[block, own]
        for m in flips:
            total = total + (r3[block, m - 1] if wide_image(m) else n3[block, m - 1].astype(F32))
        x[k, block] = total
    pair = send(x.at[k], x.at[k], pair_s.at[2], pair_v.at[2], partner)

    def image_copies(turns=(0, 1)):
        return [
            copy_of(x.at[k, core], im.at[c, k], s8.at[m - 1, n], v8.at[k, m - 1], at_col(col_peer(m), core))
            for m in flips for n, core in enumerate((k, other)) if n in turns
        ]

    piece = gp.shape[2]

    def gram(first, count):
        mine = x[k].reshape(2 * part, width)
        for n in range(count):
            full = exact(x[n].reshape(2 * part, width), mine, 0, 0)
            for to in range(groups):
                gp[to, n] = full[to * piece:(to + 1) * piece]
        some = slice(0, count)
        copies = []
        for s in range(1, groups):
            to = row_peer(s)
            copies.append(send(gp.at[to, some], ra.at[s - 1, some], s7.at[s - 1], v7.at[s - 1], at_row(to, k)))
        if first == 0:
            for copy in image_copies((0,)):
                copy.start()
        for copy in copies:
            copy.wait()
        total = gp[r, some]
        for s in range(1, groups):
            total = total + ra[s - 1, some]
        gb[c, some] = total
        copies = [send(gb.at[c, some], gb.at[c, some], s9.at[m - 1], v9.at[m - 1], at_col(col_peer(m), k)) for m in flips]
        for copy in copies:
            copy.wait()
        total = gb[0, some]
        for to in range(1, cols):
            total = total + gb[to, some]
        there = slice(first, first + count)
        gf[r, there] = total
        send(gf.at[r, there], gf.at[r, there], sf.at[0, 0], vf.at[k, 0], partner)
        for n, core in enumerate((k, other)):
            for s in range(1, groups):
                send(gf.at[r, there], gf.at[r, there], sf.at[s, n], vf.at[k, s], at_row(row_peer(s), core))
        for copy in image_copies((1,) if first == 0 else (0, 1)):
            copy.start()

    @pl.when(k == 0)
    def _():
        gram(0, 1)

    @pl.when(k == 1)
    def _():
        pair.wait_recv()
        gram(1, 2)

    def gathered(first, count):
        there = slice(first, first + count)
        source = min(first, 1)

        @pl.when(k != source)
        def _():
            arrive(gf.at[r, there], vf.at[source, 0])

        for s in range(1, groups):
            arrive(gf.at[lax.rem(r + groups - s, groups), there], vf.at[source, s])

    def whole(n):
        return jnp.concatenate([gf[g, n] for g in range(groups)], axis=0)

    gathered(0, 1)
    s0_ref[...] = whole(0)
    eliminate(s0_ref, w0_ref)
    gathered(1, 2)
    upper = exact(w0_ref[...], whole(1), 1, 0)
    s1_ref[...] = whole(2) - exact(upper, upper, 0, 0)
    cross = exact(upper, w0_ref[...], 0, 0)
    row = lax.broadcasted_iota(jnp.int32, (width, width), 0)
    col = lax.broadcasted_iota(jnp.int32, (width, width), 1)
    low, high = slice(0, width), slice(width, 2 * width)
    factor_ref[low, low] = jnp.where(row <= col, s0_ref[...], 0.0) / root
    factor_ref[low, high] = upper / root
    factor_ref[high, low] = jnp.zeros((width, width), F32)
    eliminate(s1_ref, w1_ref)
    factor_ref[high, high] = jnp.where(row <= col, s1_ref[...], 0.0) / root
    columns = inverse_ref.shape[0]
    first = c * columns
    mine = pl.ds(pl.multiple_of(lax.rem(first, width), columns), columns)
    last = w1_ref[mine, :]
    before = first < width
    inverse_ref[:, low] = jnp.where(before, w0_ref[mine, :], -exact(last, cross, 1, 0))
    inverse_ref[:, high] = jnp.where(before, 0.0, last)

    @pl.when(k == 0)
    def _():
        pair.wait_recv()

    im[c, k] = x[k, k]
    im[c, other] = x[other, k]
    for j in range(2):
        for m in flips:
            arrive(im.at[col_peer(m), j], v8.at[j, m - 1])
    for copies in first_sums:
        for copy in copies:
            copy.wait_send()
    for copy in sends:
        copy.wait_send()
    copy_of(sg.at[0], sk.at[k, c], pair_s.at[1], pair_v.at[1], partner).wait_send()
    pair.wait_send()
    for copy in image_copies():
        copy.wait_send()

    def sent(first, count):
        there = slice(first, first + count)
        copy_of(gf.at[r, there], gf.at[r, there], sf.at[0, 0], vf.at[k, 0], partner).wait_send()
        for s in range(1, groups):
            for n, core in enumerate((k, other)):
                copy_of(gf.at[r, there], gf.at[r, there], sf.at[s, n], vf.at[k, s], at_row(row_peer(s), core)).wait_send()

    @pl.when(k == 0)
    def _():
        sent(0, 1)

    @pl.when(k == 1)
    def _():
        sent(1, 2)


def basis_kernel(root, inverse_ref, im, factor_ref, basis_ref, out_ref):
    out_ref[...] = factor_ref[...]
    cols, parts, part, width = im.shape
    rows = [jnp.concatenate([im[to, n] for to in range(cols)], axis=0) for n in range(parts)]
    image = jnp.concatenate(rows, axis=1)
    size = inverse_ref.shape[0]
    left, left_rest, _ = split(inverse_ref[...])
    right, right_rest, _ = split(image)
    dims = (((1,), (1,)), ((), ()))
    both = lax.dot_general(jnp.concatenate([left, left_rest], axis=0), right, dims, preferred_element_type=F32)
    rest = lax.dot_general(left, right_rest, dims, preferred_element_type=F32)
    basis_ref[...] = (both[:size] + (both[size:] + rest)) * root


def power_step(operator, test_matrix, sizes, ratio, root):
    outer, inner, cols = sizes
    rows, depth = operator.shape
    rank = test_matrix.shape[1]
    half = rank // 2
    groups = outer * inner // 2
    part = rows // cols
    lanes = half // groups
    dma = pltpu.SemaphoreType.DMA
    vmem = pltpu.VMEM
    blocks = (2, cols - 1, part, half)
    span = depth // SPANS
    scratch = [
        vmem((2, rows, depth), BF16),
        vmem((depth, rank), BF16),
        vmem((2, rows, half), F32),
        vmem((2, rows, half), BF16),
        vmem(blocks, F32),
        vmem(blocks, BF16),
        vmem((2, part, half), BF16),
        vmem((2, cols, part, half), BF16),
        vmem((SPANS, groups, lanes, span), F32),
        vmem((SPANS, groups, lanes, span), BF16),
        vmem((SPANS, groups - 1, lanes, span), BF16),
        vmem((SPANS, groups, lanes, span), BF16),
        vmem((2, rows, half), F32),
        vmem((2, rows, half), BF16),
        vmem(blocks, F32),
        vmem(blocks, BF16),
        vmem((2, 2, part, half), F32),
        vmem((groups, 2, lanes, half), F32),
        vmem((groups - 1, 2, lanes, half), F32),
        vmem((cols, 2, lanes, half), F32),
        vmem((groups, 3, lanes, half), F32),
        vmem((half, half), F32),
        vmem((half, half), F32),
        vmem((half, half), F32),
        vmem((half, half), F32),
        dma((LOADS, 2)),
        dma((3,)), dma((3,)),
    ]
    across, along = (2, cols - 1), (SPANS, groups - 1)
    for shape in (across, across, along, along, across):
        scratch += [dma(shape), dma(shape)]
    scratch += [dma((groups - 1,)), dma((groups - 1,))]
    scratch += [dma((cols - 1, 2)), dma((2, cols - 1))]
    scratch += [dma((cols - 1,)), dma((cols - 1,))]
    scratch += [dma((groups, 2)), dma((2, groups))]
    whole = pl.BlockSpec(memory_space=pltpu.VMEM)
    inverse, image, factor = pl.pallas_call(
        functools.partial(power_kernel, sizes, ratio, root),
        out_shape=(
            jax.ShapeDtypeStruct((rank // cols, rank), F32),
            jax.ShapeDtypeStruct((cols, 2, part, half), F32),
            jax.ShapeDtypeStruct((rank, rank), F32),
        ),
        in_specs=[pl.BlockSpec(memory_space=pl.ANY)] * 2,
        out_specs=(whole,) * 3,
        scratch_shapes=scratch,
        compiler_params=pltpu.CompilerParams(
            collective_id=0, has_side_effects=True, vmem_limit_bytes=53 << 20
        ),
        name="power_step",
    )(operator, test_matrix)
    return pl.pallas_call(
        functools.partial(basis_kernel, root),
        out_shape=(
            jax.ShapeDtypeStruct((rank // cols, rows), F32),
            jax.ShapeDtypeStruct((rank, rank), F32),
        ),
        in_specs=[whole] * 3,
        out_specs=(whole,) * 2,
        compiler_params=pltpu.CompilerParams(vmem_limit_bytes=8 << 20),
        name="basis",
    )(inverse, image, factor)


def shards(operator, test_matrix):
    sizes = tuple(lax.axis_size(name) for name in ("outer", "inner", "col"))
    row_groups = sizes[0] * sizes[1]
    col_groups = sizes[2]
    total_rows = operator.shape[0] * row_groups
    total_cols = operator.shape[1] * col_groups
    root = float(total_rows) ** 0.5
    basis, factor = power_step(operator, test_matrix, sizes, total_cols / total_rows, root)
    return (basis.T, factor)


def solution(mesh):
    placed = (P(("outer", "inner"), "col"), P("col", None))
    return jax.shard_map(
        shards,
        mesh=mesh,
        in_specs=placed,
        out_specs=(P(("outer", "inner"), "col"), P()),
        check_vma=False,
    )
```

```python
import functools

import jax
import jax.numpy as jnp
from jax import lax
from jax.experimental import pallas as pl
from jax.experimental.pallas import tpu as pltpu
from jax.sharding import PartitionSpec as P

F32 = jnp.float32
BF16 = jnp.bfloat16
MESH = pl.DeviceIdType.MESH
HIGHEST = lax.Precision.HIGHEST
SPANS = 4
LOADS = 4
BLOCK = 32


def wide_sketch(half, flip):
    return flip == 1


def wide_image(flip):
    return False


def split(value):
    high = value.astype(BF16)
    rest = value - high.astype(F32)
    middle = rest.astype(BF16)
    low = (rest - middle.astype(F32)).astype(BF16)
    return high, middle, low


def eliminate(s_ref, w_ref):
    size = s_ref.shape[0]
    row = lax.broadcasted_iota(jnp.int32, (size, size), 0)
    col = lax.broadcasted_iota(jnp.int32, (size, size), 1)
    w_ref[...] = jnp.where(row == col, jnp.float32(1), jnp.float32(0))
    sub = lax.broadcasted_iota(jnp.int32, (8, 128), 0)
    wide = 128
    for start in range(0, size, BLOCK):
        rows = BLOCK // 8
        tiles = [(s_ref, t) for t in range(start // wide, size // wide)]
        tiles += [(w_ref, t) for t in range(0, start // wide + 1)]
        q = [[ref[start + 8 * g:start + 8 * g + 8, t * wide:(t + 1) * wide] for ref, t in tiles]
             for g in range(rows)]
        for p in range(rows):
            first = (start + 8 * p) % wide
            cs = [[jnp.broadcast_to(q[g][0][:, first + n:first + n + 1], (8, wide)) for n in range(8)]
                  for g in range(p, rows)]
            pivots = jnp.zeros((8, wide), F32)
            for n in range(8):
                pivot = jnp.broadcast_to(cs[0][n][n:n + 1], (8, wide))
                pivots = jnp.where(sub == n, pivot, pivots)
                inverse = 1.0 / pivot
                heads = {m: jnp.broadcast_to(cs[0][m][n:n + 1], (8, wide)) * inverse for m in range(n + 1, 8)}
                bodies = [jnp.broadcast_to(tile[n:n + 1], (8, wide)) * inverse for tile in q[p]]
                for g in range(p, rows):
                    weight = cs[g - p][n]
                    if g == p:
                        weight = jnp.where(sub > n, weight, 0.0)
                    for m in range(n + 1, 8):
                        cs[g - p][m] = cs[g - p][m] - weight * heads[m]
                    q[g] = [tile - weight * body for tile, body in zip(q[g], bodies)]
            scale = lax.rsqrt(pivots)
            q[p] = [tile * scale for tile in q[p]]
        for g in range(rows):
            for (ref, t), tile in zip(tiles, q[g]):
                ref[start + 8 * g:start + 8 * g + 8, t * wide:(t + 1) * wide] = tile
        done = start + BLOCK
        if done < size:
            block = jnp.concatenate([jnp.concatenate(q[g], axis=1) for g in range(rows)], axis=0)
            h, m, l = split(block)
            count = size // wide - start // wide
            base = (start // wide) * wide
            take = slice(done - base, count * wide) if (done - base) % wide == 0 else slice(0, count * wide)
            skip = done - base - (take.start or 0)
            left = jnp.concatenate([h, h, m, m, h, l], axis=0)[:, take]
            right = jnp.concatenate([h, m, h, m, l, h], axis=0)
            update = lax.dot_general(left, right, (((0,), (0,)), ((), ())), preferred_element_type=F32)[skip:]
            for at, (ref, t) in enumerate(tiles):
                lanes = slice(t * wide, (t + 1) * wide)
                ref[done:, lanes] = ref[done:, lanes] - update[:, at * wide:(at + 1) * wide]


def exact(left, right, left_dim, right_dim):
    return lax.dot_general(left, right, (((left_dim,), (right_dim,)), ((), ())),
                           precision=HIGHEST, preferred_element_type=F32)


def power_kernel(
    sizes, ratio, root, a_hbm, om_hbm, inverse_ref, im, factor_ref,
    a, om, p1, w1, r1, n1, sg, sk, p2, w2, r2, nt, p3, w3, r3, n3, x, gp, ra, gb, gf, s0_ref, s1_ref, w0_ref, w1_ref,
    load_sem, pair_s, pair_v, s1, v1, s2, v2, s3, v3, s4, v4, s5, v5, s7, v7, s8, v8, s9, v9, sf, vf,
):
    outer, inner, cols = sizes
    chips = inner // 2
    groups = outer * chips
    o, i, c = lax.axis_index("outer"), lax.axis_index("inner"), lax.axis_index("col")
    k = lax.rem(i, 2)
    other = 1 - k
    chip = lax.div(i, 2)
    r = o * chips + chip
    partner = (o, chip * 2 + other, c)
    flips = (2, 3, 1)

    def col_peer(m):
        return jnp.bitwise_xor(c, m)

    def row_peer(s):
        return lax.rem(r + s, groups)

    def at_col(to, core):
        return (o, chip * 2 + core, to)

    def at_row(to, core):
        return (lax.div(to, chips), lax.rem(to, chips) * 2 + core, c)

    def copy_of(src, dst, ss, rs, to):
        return pltpu.make_async_remote_copy(
            src_ref=src, dst_ref=dst, send_sem=ss, recv_sem=rs, device_id=to, device_id_type=MESH
        )

    def send(src, dst, ss, rs, to):
        copy = copy_of(src, dst, ss, rs, to)
        copy.start()
        return copy

    def arrive(dst, rs):
        copy_of(dst, dst, rs, rs, partner).wait_recv()

    width = om.shape[1] // 2

    def lanes_of(h):
        return slice(h * width, (h + 1) * width)

    depths = [slice(n * (om.shape[0] // LOADS), (n + 1) * (om.shape[0] // LOADS)) for n in range(LOADS)]
    loads = []
    for n, at in enumerate(depths):
        loads.append([
            pltpu.make_async_copy(a_hbm.at[:, at], a.at[k, :, at], load_sem.at[n, 0]),
            pltpu.make_async_copy(om_hbm.at[at], om.at[at], load_sem.at[n, 1]),
        ])
        for load in loads[n]:
            load.start()

    barrier = pltpu.get_barrier_semaphore()
    peers = [partner]
    for m in flips:
        peers += [at_col(col_peer(m), k), at_col(col_peer(m), other)]
    for s in range(1, groups):
        peers += [at_row(row_peer(s), k), at_row(row_peer(s), other)]
    for to in peers:
        pl.semaphore_signal(barrier, inc=1, device_id=to, device_id_type=MESH)

    part = p1.shape[1] // cols
    own = pl.ds(pl.multiple_of(c * part, part), part)

    def rows_of(to):
        return pl.ds(pl.multiple_of(to * part, part), part)

    sends = []
    sums = []
    for h in range(2):
        product = None
        for n, at in enumerate(depths):
            if h == 0:
                for load in loads[n]:
                    load.wait()
            term = jnp.dot(a[k, :, at], om[at, lanes_of(h)], preferred_element_type=F32)
            product = term if product is None else product + term
        p1[h] = product
        if not all(wide_sketch(h, m) for m in flips):
            w1[h] = p1[h].astype(BF16)
        if h == 0:
            pl.semaphore_wait(barrier, len(peers))
        copies = []
        for n, m in enumerate(flips):
            to = col_peer(m)
            src, dst = (p1, r1) if wide_sketch(h, m) else (w1, n1)
            copies.append(send(src.at[h, rows_of(to)], dst.at[h, m - 1], s1.at[h, m - 1], v1.at[h, m - 1], at_col(to, k)))
        sums.append(copies)
        if h == 1:
            swap = send(a_hbm, a.at[k], pair_s.at[0], pair_v.at[0], partner)
    first_sums = sums
    for h in range(2):
        for copy in sums[h]:
            copy.wait_recv()
        total = p1[h, own]
        for m in flips:
            total = total + (r1[h, m - 1] if wide_sketch(h, m) else n1[h, m - 1].astype(F32))
        sg[h] = total.astype(BF16)
        for m in flips:
            sends.append(send(sg.at[h], sk.at[k, c], s2.at[h, m - 1], v2.at[k, m - 1], at_col(col_peer(m), h)))

        @pl.when(k == h)
        def _():
            sk[k, c] = sg[h]

        @pl.when(k != h)
        def _():
            send(sg.at[h], sk.at[k, c], pair_s.at[1], pair_v.at[1], partner)

    swap.wait()
    arrive(sk.at[other, c], pair_v.at[1])
    turned = []
    for j in range(2):
        for m in flips:
            arrive(sk.at[j, col_peer(m)], v2.at[j, m - 1])
        turned.append(jnp.concatenate([sk[j, to] for to in range(cols)], axis=0).astype(F32).T.astype(BF16))
    lanes = p2.shape[2]
    depth = p2.shape[3]
    sums = []
    for span in range(SPANS):
        at = slice(span * depth, (span + 1) * depth)
        normal = None
        for j in range(2):
            term = jnp.dot(turned[j], a[j, :, at], preferred_element_type=F32)
            normal = term if normal is None else normal + term
        for g in range(groups):
            p2[span, g] = normal[g * lanes:(g + 1) * lanes]
            w2[span, g] = normal[g * lanes:(g + 1) * lanes].astype(BF16)
        copies = []
        for s in range(1, groups):
            to = row_peer(s)
            copies.append(send(w2.at[span, to], r2.at[span, s - 1], s3.at[span, s - 1], v3.at[span, s - 1], at_row(to, k)))
        sums.append(copies)
    wholes = []
    for span in range(SPANS):
        for copy in sums[span]:
            copy.wait()
        total = p2[span, r]
        for s in range(1, groups):
            total = total + r2[span, s - 1].astype(F32)
        nt[span, r] = (total * ratio).astype(BF16)
        copies = []
        for s in range(1, groups):
            copies.append(send(nt.at[span, r], nt.at[span, r], s4.at[span, s - 1], v4.at[span, s - 1], at_row(row_peer(s), k)))
        wholes.append(copies)

    spans = []
    sums = []
    for span in range(SPANS):
        for copy in wholes[span]:
            copy.wait()
        if lanes % 16 == 0:
            spans.append(nt[span].reshape(groups * lanes, depth))
        else:
            spans.append(jnp.concatenate([nt[span, g].astype(F32) for g in range(groups)], axis=0).astype(BF16))
        for block in range(2):
            term = lax.dot_general(a[block, :, span * depth:(span + 1) * depth], spans[span],
                                   (((1,), (1,)), ((), ())), preferred_element_type=F32)
            if span > 0:
                term = p3[block] + term
            p3[block] = term
            if span < SPANS - 1:
                continue
            w3[block] = term.astype(BF16)
            copies = []
            for m in flips:
                to = col_peer(m)
                src, dst = (p3, r3) if wide_image(m) else (w3, n3)
                copies.append(send(src.at[block, rows_of(to)], dst.at[block, m - 1],
                                   s5.at[block, m - 1], v5.at[block, m - 1], at_col(to, k)))
            sums.append(copies)
    for block in range(2):
        for copy in sums[block]:
            copy.wait()
        total = p3[block, own]
        for m in flips:
            total = total + (r3[block, m - 1] if wide_image(m) else n3[block, m - 1].astype(F32))
        x[k, block] = total
    pair = send(x.at[k], x.at[k], pair_s.at[2], pair_v.at[2], partner)

    def image_copies(turns=(0, 1)):
        return [
            copy_of(x.at[k, core], im.at[c, k], s8.at[m - 1, n], v8.at[k, m - 1], at_col(col_peer(m), core))
            for m in range(1, cols) for n, core in enumerate((k, other)) if n in turns
        ]

    piece = gp.shape[2]

    def gram(first, count):
        mine = x[k].reshape(2 * part, width)
        for n in range(count):
            full = exact(x[n].reshape(2 * part, width), mine, 0, 0)
            for to in range(groups):
                gp[to, n] = full[to * piece:(to + 1) * piece]
        some = slice(0, count)
        copies = []
        for s in range(1, groups):
            to = row_peer(s)
            copies.append(send(gp.at[to, some], ra.at[s - 1, some], s7.at[s - 1], v7.at[s - 1], at_row(to, k)))
        if first == 0:
            for copy in image_copies((0,)):
                copy.start()
        for copy in copies:
            copy.wait()
        total = gp[r, some]
        for s in range(1, groups):
            total = total + ra[s - 1, some]
        gb[c, some] = total
        copies = [send(gb.at[c, some], gb.at[c, some], s9.at[m - 1], v9.at[m - 1], at_col(col_peer(m), k)) for m in flips]
        for copy in copies:
            copy.wait()
        total = gb[0, some]
        for to in range(1, cols):
            total = total + gb[to, some]
        there = slice(first, first + count)
        gf[r, there] = total
        send(gf.at[r, there], gf.at[r, there], sf.at[0, 0], vf.at[k, 0], partner)
        for n, core in enumerate((k, other)):
            for s in range(1, groups):
                send(gf.at[r, there], gf.at[r, there], sf.at[s, n], vf.at[k, s], at_row(row_peer(s), core))
        for copy in image_copies((1,) if first == 0 else (0, 1)):
            copy.start()

    @pl.when(k == 0)
    def _():
        gram(0, 1)

    @pl.when(k == 1)
    def _():
        pair.wait_recv()
        gram(1, 2)

    def gathered(first, count):
        there = slice(first, first + count)
        source = min(first, 1)

        @pl.when(k != source)
        def _():
            arrive(gf.at[r, there], vf.at[source, 0])

        for s in range(1, groups):
            arrive(gf.at[lax.rem(r + groups - s, groups), there], vf.at[source, s])

    def whole(n):
        return jnp.concatenate([gf[g, n] for g in range(groups)], axis=0)

    gathered(0, 1)
    s0_ref[...] = whole(0)
    eliminate(s0_ref, w0_ref)
    gathered(1, 2)
    upper = exact(w0_ref[...], whole(1), 1, 0)
    s1_ref[...] = whole(2) - exact(upper, upper, 0, 0)
    cross = exact(upper, w0_ref[...], 0, 0)
    row = lax.broadcasted_iota(jnp.int32, (width, width), 0)
    col = lax.broadcasted_iota(jnp.int32, (width, width), 1)
    low, high = slice(0, width), slice(width, 2 * width)
    factor_ref[low, low] = jnp.where(row <= col, s0_ref[...], 0.0) / root
    factor_ref[low, high] = upper / root
    factor_ref[high, low] = jnp.zeros((width, width), F32)
    eliminate(s1_ref, w1_ref)
    factor_ref[high, high] = jnp.where(row <= col, s1_ref[...], 0.0) / root
    columns = inverse_ref.shape[0]
    first = c * columns
    mine = pl.ds(pl.multiple_of(lax.rem(first, width), columns), columns)
    last = w1_ref[mine, :]
    before = first < width
    inverse_ref[:, low] = jnp.where(before, w0_ref[mine, :], -exact(last, cross, 1, 0))
    inverse_ref[:, high] = jnp.where(before, 0.0, last)

    @pl.when(k == 0)
    def _():
        pair.wait_recv()

    im[c, k] = x[k, k]
    im[c, other] = x[other, k]
    for j in range(2):
        for m in flips:
            arrive(im.at[col_peer(m), j], v8.at[j, m - 1])
    for copies in first_sums:
        for copy in copies:
            copy.wait_send()
    for copy in sends:
        copy.wait_send()
    copy_of(sg.at[0], sk.at[k, c], pair_s.at[1], pair_v.at[1], partner).wait_send()
    pair.wait_send()
    for copy in image_copies():
        copy.wait_send()

    def sent(first, count):
        there = slice(first, first + count)
        copy_of(gf.at[r, there], gf.at[r, there], sf.at[0, 0], vf.at[k, 0], partner).wait_send()
        for s in range(1, groups):
            for n, core in enumerate((k, other)):
                copy_of(gf.at[r, there], gf.at[r, there], sf.at[s, n], vf.at[k, s], at_row(row_peer(s), core)).wait_send()

    @pl.when(k == 0)
    def _():
        sent(0, 1)

    @pl.when(k == 1)
    def _():
        sent(1, 2)


def basis_kernel(root, inverse_ref, im, factor_ref, basis_ref, out_ref):
    out_ref[...] = factor_ref[...]
    cols, parts, part, width = im.shape
    rows = [jnp.concatenate([im[to, n] for to in range(cols)], axis=0) for n in range(parts)]
    image = jnp.concatenate(rows, axis=1)
    size = inverse_ref.shape[0]
    left, left_rest, _ = split(inverse_ref[...])
    right, right_rest, _ = split(image)
    dims = (((1,), (1,)), ((), ()))
    both = lax.dot_general(jnp.concatenate([left, left_rest], axis=0), right, dims, preferred_element_type=F32)
    rest = lax.dot_general(left, right_rest, dims, preferred_element_type=F32)
    basis_ref[...] = (both[:size] + (both[size:] + rest)) * root


def power_step(operator, test_matrix, sizes, ratio, root):
    outer, inner, cols = sizes
    rows, depth = operator.shape
    rank = test_matrix.shape[1]
    half = rank // 2
    groups = outer * inner // 2
    part = rows // cols
    lanes = half // groups
    dma = pltpu.SemaphoreType.DMA
    vmem = pltpu.VMEM
    blocks = (2, cols - 1, part, half)
    span = depth // SPANS
    scratch = [
        vmem((2, rows, depth), BF16),
        vmem((depth, rank), BF16),
        vmem((2, rows, half), F32),
        vmem((2, rows, half), BF16),
        vmem(blocks, F32),
        vmem(blocks, BF16),
        vmem((2, part, half), BF16),
        vmem((2, cols, part, half), BF16),
        vmem((SPANS, groups, lanes, span), F32),
        vmem((SPANS, groups, lanes, span), BF16),
        vmem((SPANS, groups - 1, lanes, span), BF16),
        vmem((SPANS, groups, lanes, span), BF16),
        vmem((2, rows, half), F32),
        vmem((2, rows, half), BF16),
        vmem(blocks, F32),
        vmem(blocks, BF16),
        vmem((2, 2, part, half), F32),
        vmem((groups, 2, lanes, half), F32),
        vmem((groups - 1, 2, lanes, half), F32),
        vmem((cols, 2, lanes, half), F32),
        vmem((groups, 3, lanes, half), F32),
        vmem((half, half), F32),
        vmem((half, half), F32),
        vmem((half, half), F32),
        vmem((half, half), F32),
        dma((LOADS, 2)),
        dma((3,)), dma((3,)),
    ]
    across, along = (2, cols - 1), (SPANS, groups - 1)
    for shape in (across, across, along, along, across):
        scratch += [dma(shape), dma(shape)]
    scratch += [dma((groups - 1,)), dma((groups - 1,))]
    scratch += [dma((cols - 1, 2)), dma((2, cols - 1))]
    scratch += [dma((cols - 1,)), dma((cols - 1,))]
    scratch += [dma((groups, 2)), dma((2, groups))]
    whole = pl.BlockSpec(memory_space=pltpu.VMEM)
    inverse, image, factor = pl.pallas_call(
        functools.partial(power_kernel, sizes, ratio, root),
        out_shape=(
            jax.ShapeDtypeStruct((rank // cols, rank), F32),
            jax.ShapeDtypeStruct((cols, 2, part, half), F32),
            jax.ShapeDtypeStruct((rank, rank), F32),
        ),
        in_specs=[pl.BlockSpec(memory_space=pl.ANY)] * 2,
        out_specs=(whole,) * 3,
        scratch_shapes=scratch,
        compiler_params=pltpu.CompilerParams(
            collective_id=0, has_side_effects=True, vmem_limit_bytes=53 << 20
        ),
        name="power_step",
    )(operator, test_matrix)
    return pl.pallas_call(
        functools.partial(basis_kernel, root),
        out_shape=(
            jax.ShapeDtypeStruct((rank // cols, rows), F32),
            jax.ShapeDtypeStruct((rank, rank), F32),
        ),
        in_specs=[whole] * 3,
        out_specs=(whole,) * 2,
        compiler_params=pltpu.CompilerParams(vmem_limit_bytes=8 << 20),
        name="basis",
    )(inverse, image, factor)


def shards(operator, test_matrix):
    sizes = tuple(lax.axis_size(name) for name in ("outer", "inner", "col"))
    row_groups = sizes[0] * sizes[1]
    col_groups = sizes[2]
    total_rows = operator.shape[0] * row_groups
    total_cols = operator.shape[1] * col_groups
    root = float(total_rows) ** 0.5
    basis, factor = power_step(operator, test_matrix, sizes, total_cols / total_rows, root)
    return (basis.T, factor)


def solution(mesh):
    placed = (P(("outer", "inner"), "col"), P("col", None))
    return jax.shard_map(
        shards,
        mesh=mesh,
        in_specs=placed,
        out_specs=(P(("outer", "inner"), "col"), P()),
        check_vma=False,
    )
```
